32 devices in a mesh: wide: 8 (over z, y), narrow: 4 (over x, core).
Axes of the slice: x: 2, y: 2, z: 4, core: 2. Of those that a mesh axis runs over, the one named last changes fastest.
Arguments:
- inputs: bfloat16 [4, 1024, 1536], P('narrow', 'wide'), may hold values from -6 to 6
- out_grad: bfloat16 [4, 1024, 1536], P('narrow', 'wide'), may hold values from -6 to 6
- qkv_w: float32 [3, 1536, 1536], P(None, ('wide', 'narrow')), may hold values from -0.15625 to 0.15625
- out_w: float32 [1536, 1536], P(('wide', 'narrow')), may hold values from -0.875 to 0.875
- ffn_in: float32 [2, 1536, 4096], P(None, None, ('wide', 'narrow')), may hold values from -0.15625 to 0.15625
- ffn_out: float32 [4096, 1536], P(('wide', 'narrow')), may hold values from -0.09375 to 0.09375
- qkv_mom: float32 [3, 1536, 1536], P(None, ('wide', 'narrow')), may hold values from -0.0012207031 to 0.0012207031
- out_mom: float32 [1536, 1536], P(('wide', 'narrow')), may hold values from -0.0012207031 to 0.0012207031
- in_mom: float32 [2, 1536, 4096], P(None, None, ('wide', 'narrow')), may hold values from -0.0012207031 to 0.0012207031
- down_mom: float32 [4096, 1536], P(('wide', 'narrow')), may hold values from -0.0012207031 to 0.0012207031
- gains: float32 [2, 1536], replicated, may hold values from 0.5 to 1.5
- gains_m: float32 [2, 1536], replicated, may hold values from -0.00048828125 to 0.00048828125
- gains_v: float32 [2, 1536], replicated, may hold values from 1.4108595e-08 to 2.469004e-07
- fgate_w: float32 [1536, 24], replicated, may hold values from -0.15625 to 0.15625
- fgate_w_m: float32 [1536, 24], replicated, may hold values from -0.00012207031 to 0.00012207031
- fgate_w_v: float32 [1536, 24], replicated, may hold values from 9.1705865e-10 to 1.4814025e-08
- fgate_b: float32 [24], replicated, may hold values from 3 to 10
- fgate_b_m: float32 [24], replicated, may hold values from -0.0012207031 to 0.0012207031
- fgate_b_v: float32 [24], replicated, may hold values from 9.1705864e-08 to 1.4814025e-06
- doc_ids: int32 [4, 1024], P('narrow'), may hold values from 0 to 2, never falling along the last dimension, each value on 1 to 512 neighbouring positions
- group_ids: int32 [4, 16], P('narrow'), may hold values from 0 to 15, as said below
- block_mask: int32 [4, 16, 16], P('narrow'), may hold values 0 or 1
Outputs:
- output: bfloat16 [4, 1024, 1536], P('narrow', 'wide')
- grad_inputs: float32 [4, 1024, 1536], P('narrow', 'wide')
- grad_norm: float32 [1], replicated
- new_qkv_w: float32 [3, 1536, 1536], P(None, ('wide', 'narrow'))
- new_out_w: float32 [1536, 1536], P(('wide', 'narrow'))
- new_ffn_in: float32 [2, 1536, 4096], P(None, None, ('wide', 'narrow'))
- new_ffn_out: float32 [4096, 1536], P(('wide', 'narrow'))
- new_qkv_mom: float32 [3, 1536, 1536], P(None, ('wide', 'narrow'))
- new_out_mom: float32 [1536, 1536], P(('wide', 'narrow'))
- new_in_mom: float32 [2, 1536, 4096], P(None, None, ('wide', 'narrow'))
- new_down_mom: float32 [4096, 1536], P(('wide', 'narrow'))
- new_gains: float32 [2, 1536], replicated
- new_gains_m: float32 [2, 1536], replicated
- new_gains_v: float32 [2, 1536], replicated
- new_fgate_w: float32 [1536, 24], replicated
- new_fgate_w_m: float32 [1536, 24], replicated
- new_fgate_w_v: float32 [1536, 24], replicated
- new_fgate_b: float32 [24], replicated
- new_fgate_b_m: float32 [24], replicated
- new_fgate_b_v: float32 [24], replicated
The draws below stay inside these ranges and needn't reach their ends.
Inputs may be any that keep to these rules, and one draw needn't show every extreme that they name: `group_ids`: in every sequence, slots 2w and 2w + 1 hold groups p(w) and 15 - p(w) for a permutation p of 0 to 7; every group is held once.
All inputs are finite; a program needn't handle non-finite values. No bound on the sum of `block_mask` on one device may be relied on, other than what follows from the above.
Results may differ from the reference program's by a relative error of at most 0.028.
Values may be sent and summed in bfloat16 or wider, within the bound.
No kernel may reach another device: no remote copies, remote signals or barrier semaphores. Data moves between devices by JAX's collectives and lax.ppermute only.
A program may use at most 448 MiB of HBM per device.

```python
import math
import jax
import jax.numpy as jnp
import numpy as np
from jax import lax

D = 1536
H = 24
DH = 64
FF = 4096
TOK_DEV = 128
SWEEPS = 5
STEP = 10
CH = 64
NTOK = 1024
NCH = 16
SEQS = 4
LMAX = 512
NDOC = 3
NPARAM = 28351512


def draw_group_ids(key, part):
    subkeys = jax.random.split(key, SEQS)

    def one_sequence(subkey):
        leading = jax.random.permutation(subkey, NCH // 2).astype(jnp.int32)
        return jnp.stack([leading, NCH - 1 - leading], axis=1).reshape(NCH)
    return jax.vmap(one_sequence)(subkeys)


def with_ends(entries, own_key, least, largest):
    longest = entries.shape.index(max(entries.shape))
    spots = []
    for shift in (0, 1):
        where = [jax.random.randint(jax.random.fold_in(own_key, axis), (), 0, length) for axis, length in enumerate(entries.shape)]
        where[longest] = (where[longest] + shift) % entries.shape[longest]
        spots.append(tuple(where))
    return entries.at[spots[0]].set(least).at[spots[1]].set(largest)


def levels(rng, extent, shards, low, top_value):
    def one(dim, blocks):
        draws = jax.random.uniform(jax.random.fold_in(jax.random.fold_in(rng, 6), dim), (blocks,), jnp.float32, low / len(shards), top_value / len(shards))
        return jnp.repeat(jnp.exp(draws), extent[dim] // blocks).reshape((-1,) + (1,) * (len(extent) - dim - 1))

    level = one(*shards[0])
    for cut in shards[1:]:
        level = level * one(*cut)
    return level


def split_up(number_of, total, most, skew):
    loads = [(1 << 20) // math.isqrt(grade ** skew) + 1 for grade in range(2, number_of + 1)]
    surplus, counts = total - most - (number_of - 1), [1] * (number_of - 1)
    while surplus > 0:
        candidates = [i for i in range(number_of - 1) if counts[i] < most]
        whole, budget = sum([loads[i] for i in candidates]), surplus
        for i in candidates:
            extra = min(most - counts[i], max(1, budget * loads[i] // whole), surplus)
            counts[i] = counts[i] + extra
            surplus = surplus - extra
    return np.array([most] + counts)


def ragged_sizes(stream_key, number_of, total, reach, skew):
    if number_of == 2:
        one = jax.random.randint(stream_key, (), max(1, total - reach), min(reach, total - 1) + 1)
        return jnp.stack([one, total - one])
    sizes = jnp.asarray(split_up(number_of, total, reach, skew), jnp.int32)
    couples = (number_of - 1) // 2
    source_of, taker = sizes[1:1 + 2 * couples:2], sizes[2:2 + 2 * couples:2]
    margin = jnp.minimum(source_of - 1, reach - taker)
    passed = jax.random.randint(jax.random.fold_in(stream_key, 1), (couples,), 0, 1 << 20) % (margin + 1)
    sizes = sizes.at[1:1 + 2 * couples:2].set(source_of - passed).at[2:2 + 2 * couples:2].set(taker + passed)
    return sizes[jax.random.permutation(jax.random.fold_in(stream_key, 2), number_of)]


def gaussian(own_key, shape, spread, most, shards=(), kind=jnp.bfloat16):
    factor_of = levels(own_key, shape, shards, -0.22, 0.18) if shards else 1.0
    array = jax.random.normal(own_key, shape, jnp.float32) * spread * factor_of
    return jnp.minimum(jnp.maximum(array, -most), most).astype(kind)


def setup_inputs(seed: int = 0) -> dict:
    key_of = jax.random.split(jax.random.key(seed), 23)
    inputs = gaussian(key_of[0], (SEQS, NTOK, D), 1.0, 6.0, ((0, 4), (1, 8)))
    out_grad = gaussian(key_of[1], (SEQS, NTOK, D), 1.0, 6.0, ((0, 4), (1, 8)))
    qkv_w = gaussian(key_of[2], (3, D, D), D ** -0.5, 0.15625, ((1, 32),), jnp.float32)
    out_w = gaussian(key_of[3], (D, D), (D // 32) ** -0.5, 0.875, ((0, 32),), jnp.float32)
    ffn_in = gaussian(key_of[4], (2, D, FF), D ** -0.5, 0.15625, ((2, 32),), jnp.float32)
    ffn_out = gaussian(key_of[5], (FF, D), FF ** -0.5, 0.09375, ((0, 32),), jnp.float32)
    qkv_mom = gaussian(key_of[6], (3, D, D), (NPARAM ** -0.5), 0.0012207031, ((1, 32),), jnp.float32)
    out_mom = gaussian(key_of[7], (D, D), (NPARAM ** -0.5), 0.0012207031, ((0, 32),), jnp.float32)
    in_mom = gaussian(key_of[8], (2, D, FF), (NPARAM ** -0.5), 0.0012207031, ((2, 32),), jnp.float32)
    down_mom = gaussian(key_of[9], (FF, D), (NPARAM ** -0.5), 0.0012207031, ((0, 32),), jnp.float32)
    gains = jnp.clip(1.0 + 0.1 * jax.random.normal(key_of[10], (2, D), jnp.float32), 0.5, 1.5)
    gains_m = gaussian(key_of[11], (2, D), (0.4 * NPARAM ** -0.5), 0.00048828125, (), jnp.float32)
    gains_v = jnp.clip(jnp.exp(jax.random.uniform(key_of[12], (2, D), jnp.float32, math.log(1.410859518102825e-08), math.log(2.469004130034591e-07))), 1.410859518102825e-08, 2.469004130034591e-07)
    fgate_w = gaussian(key_of[13], (D, H), D ** -0.5, 0.15625, (), jnp.float32)
    fgate_w_m = gaussian(key_of[14], (D, H), (0.11 * NPARAM ** -0.5), 0.00012207031, (), jnp.float32)
    fgate_w_v = jnp.clip(jnp.exp(jax.random.uniform(key_of[15], (D, H), jnp.float32, math.log(9.170586512396994e-10), math.log(1.4814024673626136e-08))), 9.170586512396994e-10, 1.4814024673626136e-08)
    fgate_b = jnp.clip(jax.random.uniform(key_of[16], (H,), jnp.float32, 3.0, 10.0), 3.0, 10.0)
    fgate_b_m = gaussian(key_of[17], (H,), (1.1 * NPARAM ** -0.5), 0.0012207031, (), jnp.float32)
    fgate_b_v = jnp.clip(jnp.exp(jax.random.uniform(key_of[18], (H,), jnp.float32, math.log(9.170586423579152e-08), math.log(1.4814024780207546e-06))), 9.170586423579152e-08, 1.4814024780207546e-06)
    doc_ids = jax.vmap(lambda own: jnp.searchsorted(jnp.cumsum(ragged_sizes(own, NDOC, NTOK, LMAX, 1)), jnp.arange(NTOK), side="right"))(jax.random.split(key_of[19], SEQS)).reshape((SEQS, NTOK)).astype(jnp.int32)
    group_ids = draw_group_ids(jax.random.fold_in(key_of[22], 71), 0)
    block_mask = with_ends((jax.random.randint(key_of[21], (SEQS, NCH, NCH), 0, 4) < 3).astype(jnp.int32), jax.random.fold_in(key_of[21], 1), 0, 1)
    return {"inputs": inputs, "out_grad": out_grad, "qkv_w": qkv_w, "out_w": out_w, "ffn_in": ffn_in, "ffn_out": ffn_out, "qkv_mom": qkv_mom, "out_mom": out_mom, "in_mom": in_mom, "down_mom": down_mom, "gains": gains, "gains_m": gains_m, "gains_v": gains_v, "fgate_w": fgate_w, "fgate_w_m": fgate_w_m, "fgate_w_v": fgate_w_v, "fgate_b": fgate_b, "fgate_b_m": fgate_b_m, "fgate_b_v": fgate_b_v, "doc_ids": doc_ids, "group_ids": group_ids, "block_mask": block_mask}


NORM_EPSILON = 1e-06
MASKED_SCORE = -1e+30
COEF_LINEAR = 3.4445
COEF_CUBIC = -4.775
COEF_QUINTIC = 2.0315
MOMENTUM = 0.95
MUON_DECAY = 0.01
MUON_RATE = 0.5
BETA_FIRST = 0.9
BETA_SECOND = 0.95
ADAM_EPSILON = 1e-08
ADAM_DECAY = 0.1
RATE_GAINS = 1.0
RATE_FGATE_W = 0.03
RATE_FGATE_B = 4.0
CLIP_NORM = 1.0
HIGHEST = lax.Precision.HIGHEST

@jax.custom_vjp
def low(v):
    return lax.optimization_barrier(v.astype(jnp.bfloat16)).astype(jnp.float32)

@jax.custom_vjp
def low_back(v):
    return v

def low_keep(v):
    return (low(v), None)

def low_pass(kept, grad):
    return (grad,)

def back_keep(v):
    return (v, None)

def back_low(kept, grad):
    return (low(grad),)
low.defvjp(low_keep, low_pass)
low_back.defvjp(back_keep, back_low)

def matmul(left, right):
    return jnp.dot(left, right, precision=HIGHEST, preferred_element_type=jnp.float32)

def rms_norm(hidden, gain):
    return hidden * lax.rsqrt(lax.optimization_barrier(jnp.mean(hidden * hidden, axis=-1, keepdims=True)) + NORM_EPSILON) * gain

def segment_cumsum(values, starts):
    flags = jnp.broadcast_to(starts[:, None], values.shape)

    def combine(earlier, later):
        return (jnp.where(later[1], later[0], earlier[0] + later[0]), earlier[1] | later[1])
    summed, _ = lax.associative_scan(combine, (values, flags))
    return summed

def attention(queries, keys, values, cum_rows, pos_rows, doc_rows, group_rows, allow_table):
    blocks = queries.shape[0] // TOK_DEV
    keys3 = keys.reshape(-1, H, DH)
    values3 = values.reshape(-1, H, DH)

    @jax.checkpoint
    def one_block(element):
        block_queries, block_cum, block_pos, block_doc, block_group = element
        raw = jnp.einsum('ihd,jhd->hij', block_queries, keys3, precision=HIGHEST, preferred_element_type=jnp.float32)
        scores = low_back(raw * DH ** (-0.5) + block_cum.T[:, :, None] - cum_rows.T[:, None, :])
        allowed = (pos_rows[None, :] <= block_pos[:, None]) & (doc_rows[None, :] == block_doc[:, None]) & allow_table[block_group][:, group_rows]
        scores = jnp.where(allowed[None], scores, MASKED_SCORE)
        shifted = jnp.exp(scores - lax.optimization_barrier(jnp.max(scores, axis=2, keepdims=True)))
        probs = low(shifted / lax.optimization_barrier(jnp.sum(shifted, axis=2, keepdims=True)))
        return jnp.einsum('hij,jhd->ihd', probs, values3, precision=HIGHEST, preferred_element_type=jnp.float32)
    outputs = lax.map(one_block, (queries.reshape(blocks, TOK_DEV, H, DH), cum_rows.reshape(blocks, TOK_DEV, H), pos_rows.reshape(blocks, TOK_DEV), doc_rows.reshape(blocks, TOK_DEV), group_rows.reshape(blocks, TOK_DEV)))
    return outputs.reshape(queries.shape[0], H * DH)

def layer(resid_in, params, indices):
    w_qkv3, w_out, w_in2, w_down, gain_pair, w_fgate, b_fgate = params
    starts, order_rows, pos_rows, doc_rows, group_rows, allow_table = indices
    normed = low(rms_norm(resid_in, gain_pair[0]))
    queries = low(low_back(matmul(normed, low(w_qkv3[0]))))
    keys = low(low_back(matmul(normed, low(w_qkv3[1]))))
    values = low(low_back(matmul(normed, low(w_qkv3[2]))))
    logits = low_back(matmul(normed, low(w_fgate)) + b_fgate)
    log_forget = jax.nn.log_sigmoid(logits)
    cum_seq = segment_cumsum(log_forget[order_rows], starts)
    cum_rows = cum_seq[pos_rows]
    mixed = low(low_back(attention(queries, keys, values, cum_rows, pos_rows, doc_rows, group_rows, allow_table)))
    middle = resid_in + low_back(matmul(mixed, low(w_out)))
    normed_two = low(rms_norm(middle, gain_pair[1]))
    gate_value = low_back(matmul(normed_two, low(w_in2[0])))
    up_value = low_back(matmul(normed_two, low(w_in2[1])))
    hidden = low(low_back(jax.nn.silu(gate_value) * up_value))
    return middle + low_back(matmul(hidden, low(w_down)))

def muon_step(gradient, moment, weight, step_rate):
    new_moment = MOMENTUM * moment + gradient
    direction = gradient + MOMENTUM * new_moment
    ortho = low(direction / (jnp.sqrt(jnp.sum(direction * direction)) + 1e-07))
    for sweep_number in range(SWEEPS):
        gram_block = matmul(ortho.T, ortho)
        square = matmul(ortho.T, low(matmul(ortho, low(gram_block))))
        ortho = low(COEF_LINEAR * ortho + matmul(ortho, low(COEF_CUBIC * gram_block + COEF_QUINTIC * square)))
    return ((1.0 - MUON_DECAY) * weight - step_rate * ortho, new_moment)

def adam_update(weight, first, second, gradient, bias_one, bias_two, step_rate):
    new_first = BETA_FIRST * first + (1.0 - BETA_FIRST) * gradient
    new_second = BETA_SECOND * second + (1.0 - BETA_SECOND) * gradient * gradient
    update = new_first / bias_one / (jnp.sqrt(new_second / bias_two) + ADAM_EPSILON)
    return (weight - step_rate * (update + ADAM_DECAY * weight), new_first, new_second)

def tall_rate(rows_count, cols_count, fan_in):
    return MUON_RATE * math.sqrt(max(rows_count, cols_count) / fan_in)

def reference(inputs, out_grad, qkv_w, out_w, ffn_in, ffn_out, qkv_mom, out_mom, in_mom, down_mom, gains, gains_m, gains_v, fgate_w, fgate_w_m, fgate_w_v, fgate_b, fgate_b_m, fgate_b_v, doc_ids, group_ids, block_mask):
    index_list = []
    for sequence in range(SEQS):
        slot_ids = group_ids[sequence]
        documents = doc_ids[sequence]
        starts = jnp.concatenate([jnp.ones((1,), jnp.bool_), documents[1:] != documents[:-1]])
        pos_rows = (slot_ids[:, None] * CH + jnp.arange(CH, dtype=jnp.int32)[None, :]).reshape(NTOK).astype(jnp.int32)
        order_rows = jnp.argsort(pos_rows).astype(jnp.int32)
        group_rows = jnp.repeat(slot_ids, CH)
        allow_table = jnp.eye(NCH, dtype=jnp.bool_) | (block_mask[sequence] == 1)
        index_list.append((starts, order_rows, pos_rows, documents[pos_rows], group_rows, allow_table))

    def forward(resid, w_qkv3, w_out, w_in2, w_down, gain_pair, w_fgate, b_fgate):
        params = (w_qkv3, w_out, w_in2, w_down, gain_pair, w_fgate, b_fgate)
        return jnp.stack([layer(resid[sequence], params, index_list[sequence]) for sequence in range(SEQS)])
    result, pullback = jax.vjp(forward, inputs.astype(jnp.float32), qkv_w, out_w, ffn_in, ffn_out, gains, fgate_w, fgate_b)
    grads = pullback(out_grad.astype(jnp.float32))
    grad_input, grad_qkv, grad_out, grad_in, grad_down, grad_gains, grad_fw, grad_fb = grads
    leaves = [grad_qkv, grad_out, grad_in, grad_down, grad_gains, grad_fw, grad_fb]
    grad_norm = jnp.sqrt(sum((jnp.sum(leaf * leaf) for leaf in leaves)))
    clip_factor = jnp.minimum(1.0, CLIP_NORM / (grad_norm + 1e-06))
    new_qkv_list = []
    new_qkv_moms = []
    for number in range(3):
        weight_new, moment_new = muon_step(clip_factor * grad_qkv[number], qkv_mom[number], qkv_w[number], tall_rate(D, D, D))
        new_qkv_list.append(weight_new)
        new_qkv_moms.append(moment_new)
    new_out, new_out_mom = muon_step(clip_factor * grad_out, out_mom, out_w, tall_rate(D, D, D // 32))
    new_in_list = []
    new_in_moms = []
    for number in range(2):
        weight_new, moment_new = muon_step(clip_factor * grad_in[number].T, in_mom[number].T, ffn_in[number].T, tall_rate(FF, D, D))
        new_in_list.append(weight_new.T)
        new_in_moms.append(moment_new.T)
    new_down, new_down_mom = muon_step(clip_factor * grad_down, down_mom, ffn_out, tall_rate(FF, D, FF))
    bias_one = 1.0 - BETA_FIRST ** STEP
    bias_two = 1.0 - BETA_SECOND ** STEP
    gains_new, gains_first, gains_second = adam_update(gains, gains_m, gains_v, clip_factor * grad_gains, bias_one, bias_two, RATE_GAINS)
    forget_w_new, forget_w_first, forget_w_second = adam_update(fgate_w, fgate_w_m, fgate_w_v, clip_factor * grad_fw, bias_one, bias_two, RATE_FGATE_W)
    forget_b_new, forget_b_first, forget_b_second = adam_update(fgate_b, fgate_b_m, fgate_b_v, clip_factor * grad_fb, bias_one, bias_two, RATE_FGATE_B)
    return (result.astype(jnp.bfloat16), grad_input, grad_norm.reshape(1), jnp.stack(new_qkv_list), new_out, jnp.stack(new_in_list), new_down, jnp.stack(new_qkv_moms), new_out_mom, jnp.stack(new_in_moms), new_down_mom, gains_new, gains_first, gains_second, forget_w_new, forget_w_first, forget_w_second, forget_b_new, forget_b_first, forget_b_second)
```

```python
import math

import jax
import jax.numpy as jnp
from jax import lax
from jax.sharding import PartitionSpec as P

D = 1536
H = 24
DH = 64
FF = 4096
SWEEPS = 5
STEP = 10
CH = 64


NORM_EPSILON = 1e-06
MASKED_SCORE = -1e30
COEF_LINEAR = 3.4445
COEF_CUBIC = -4.775
COEF_QUINTIC = 2.0315
MOMENTUM = 0.95
MUON_DECAY = 0.01
MUON_RATE = 0.5
BETA_FIRST = 0.9
BETA_SECOND = 0.95
ADAM_EPSILON = 1e-08
ADAM_DECAY = 0.1
RATE_GAINS = 1.0
RATE_FGATE_W = 0.03
RATE_FGATE_B = 4.0
CLIP_NORM = 1.0


def rms_parts(hidden):
    factor = lax.rsqrt(jnp.mean(hidden * hidden, axis=-1, keepdims=True) + NORM_EPSILON)
    return (hidden * factor, factor)


def rms_back(grad_normed, gain, normed, factor):
    scaled = grad_normed * gain
    return factor * (scaled - normed * jnp.mean(scaled * normed, axis=-1, keepdims=True))


def matmul_first(left, right):
    return lax.dot_general(
        left, right, (((0,), (0,)), ((), ())), preferred_element_type=jnp.float32
    )


def matmul_last(left, right):
    return lax.dot_general(
        left, right, (((1,), (1,)), ((), ())), preferred_element_type=jnp.float32
    )


def adam_update(weight, first, second, gradient, bias_one, bias_two, step_rate):
    new_first = BETA_FIRST * first + (1.0 - BETA_FIRST) * gradient
    new_second = BETA_SECOND * second + (1.0 - BETA_SECOND) * gradient * gradient
    update = new_first / bias_one / (jnp.sqrt(new_second / bias_two) + ADAM_EPSILON)
    return (weight - step_rate * (update + ADAM_DECAY * weight), new_first, new_second)


def tall_rate(rows_count, cols_count, fan_in):
    return MUON_RATE * math.sqrt(max(rows_count, cols_count) / fan_in)


def open_sum(mask, values):
    high = lax.reduce_precision(values, 8, 7)
    rest = values - high
    mid = lax.reduce_precision(rest, 8, 7)
    low = rest - mid
    count = values.shape[1]
    terms = jnp.concatenate([high, mid, low], axis=1).astype(jnp.bfloat16)
    sums = jnp.dot(mask, terms, preferred_element_type=jnp.float32)
    return sums[:, :count] + sums[:, count : 2 * count] + sums[:, 2 * count :]


def to_groups(chunks, first, rank, count):
    total = chunks.shape[0]
    received = []
    for shift in range(count):
        pick = jnp.clip((rank + shift) % count - first, 0, total - 1)
        chunk = lax.dynamic_index_in_dim(chunks, pick, 0, keepdims=False)
        if shift:
            pairs = [
                (place, (place + shift) % count)
                for place in range(count)
                if first <= (place + shift) % count < first + total
            ]
            chunk = lax.ppermute(chunk, "wide", pairs)
        received.append(chunk)
    return jnp.stack(received)


def from_groups(blocks, first, total, rank, count):
    received = []
    for shift in range(count):
        block = blocks[shift]
        if shift:
            pairs = [(place, (place - shift) % count) for place in range(first, first + total)]
            block = lax.ppermute(block, "wide", pairs)
        received.append(block)
    stacked = jnp.stack(received)
    return [
        lax.dynamic_index_in_dim(stacked, (first + k - rank) % count, 0, keepdims=False)
        for k in range(total)
    ]


def exchange(blocks):
    return lax.all_to_all(blocks, "wide", 0, 0, tiled=True)


def small_dot(left, right):
    return jnp.dot(
        left.astype(jnp.bfloat16), right.astype(jnp.bfloat16), preferred_element_type=jnp.float32
    )


def orthogonal_factor(gram):
    side = gram.shape[0]
    eye = jnp.eye(side, dtype=jnp.float32)
    factor = None
    for sweep in range(SWEEPS):
        mean = jnp.sum(gram * eye) / side
        rest = gram - mean * eye
        squared = small_dot(rest, rest)
        lead = COEF_LINEAR + COEF_CUBIC * mean + COEF_QUINTIC * mean * mean
        step = (COEF_CUBIC + 2.0 * COEF_QUINTIC * mean) * rest + COEF_QUINTIC * squared
        if sweep + 1 < SWEEPS:
            half = lead * gram + small_dot(gram, step)
            gram = lead * half + small_dot(half, step)
        if factor is None:
            factor = lead * eye + step
        else:
            factor = lead * factor + small_dot(factor, step)
    return factor


def shards(
    inputs,
    out_grad,
    qkv_w,
    out_w,
    ffn_in,
    ffn_out,
    qkv_mom,
    out_mom,
    in_mom,
    down_mom,
    gains,
    gains_m,
    gains_v,
    fgate_w,
    fgate_w_m,
    fgate_w_v,
    fgate_b,
    fgate_b_m,
    fgate_b_v,
    doc_ids,
    group_ids,
    block_mask,
):
    rank = lax.axis_index("wide")
    wide_count = lax.axis_size("wide")
    narrow_count = lax.axis_size("narrow")
    tokens = inputs.shape[1]
    seq_len = doc_ids.shape[1]
    slots = group_ids.shape[1]
    heads = -(-H // wide_count)
    head_cols = heads * DH
    padded = wide_count * head_cols
    in_rows = qkv_w.shape[1]
    ff_rows = ffn_out.shape[0]
    part_rows = D // wide_count
    scale = DH ** (-0.5)
    bf = jnp.bfloat16
    f32 = jnp.float32

    def own_tokens(array):
        return lax.dynamic_slice_in_dim(array, rank * tokens, tokens, 0)

    all_inputs = lax.all_gather(inputs[0], "wide", axis=0, tiled=True)
    qkv_cut = jnp.pad(qkv_w.astype(bf), ((0, 0), (0, 0), (0, padded - D)))
    qkv_cut = qkv_cut.reshape(3, in_rows, wide_count, head_cols).transpose(2, 0, 1, 3)
    qkv_cut = exchange(qkv_cut)
    qkv_all = lax.all_gather(qkv_cut, "narrow", axis=1)
    w_qkv = qkv_all.transpose(0, 1, 3, 2, 4).reshape(D, 3 * head_cols)
    w_out = lax.all_gather(out_w.astype(bf), ("wide", "narrow"), axis=0, tiled=True)
    w_in = lax.all_gather(ffn_in.astype(bf), "narrow", axis=2, tiled=True)
    w_down = lax.all_gather(ffn_out.astype(bf), "narrow", axis=0, tiled=True)
    all_out_grad = lax.all_gather(out_grad[0], "wide", axis=0, tiled=True)

    padding = padded // DH - H
    gate_w = lax.dynamic_slice_in_dim(
        jnp.pad(fgate_w.astype(bf), ((0, 0), (0, padding))), rank * heads, heads, 1
    )
    gate_b = lax.dynamic_slice_in_dim(jnp.pad(fgate_b, ((0, padding),)), rank * heads, heads, 0)

    slot_ids = group_ids[0]
    within = jnp.arange(CH, dtype=jnp.int32)
    place = (slot_ids[:, None] * CH + within[None, :]).reshape(seq_len)
    row_slot = jnp.repeat(slot_ids, CH)
    one_hot = (row_slot[:, None] == jnp.arange(slots)[None, :]).astype(bf)
    slot_hot = (slot_ids[:, None] == jnp.arange(slots)[None, :]).astype(bf)
    docs = jnp.dot(
        slot_hot, doc_ids[0].reshape(slots, CH).astype(bf), preferred_element_type=f32
    ).reshape(seq_len)
    allowed = jnp.eye(slots, dtype=bf) + (block_mask[0] == 1).astype(bf)
    row_allow = jnp.dot(one_hot, allowed, preferred_element_type=f32).astype(bf)
    same_doc = docs[:, None] == docs[None, :]
    before = same_doc & (place[None, :] <= place[:, None])
    before_f = before.astype(bf)

    resid = all_inputs.astype(f32)
    normed_one, _ = rms_parts(resid)
    attn_in = (normed_one * gains[0]).astype(bf)
    projected = jnp.dot(attn_in, w_qkv, preferred_element_type=f32).astype(bf)
    q_heads, k_heads, v_heads = (
        projected[:, k * head_cols : (k + 1) * head_cols]
        .reshape(seq_len, heads, DH)
        .transpose(1, 0, 2)
        for k in range(3)
    )
    logits = jnp.dot(attn_in, gate_w, preferred_element_type=f32) + gate_b
    log_forget = jax.nn.log_sigmoid(logits)
    cumulative = open_sum(before_f, log_forget)
    cum_cols = cumulative.T

    block = min(seq_len, 1024)

    def masked_scores(first):
        rows = slice(first, first + block)
        ok = before[rows] & (
            jnp.dot(row_allow[rows], one_hot.T, preferred_element_type=f32) > 0.5
        )
        raw = jnp.einsum("hid,hjd->hij", q_heads[:, rows], k_heads, preferred_element_type=f32)
        scores = raw * scale + cum_cols[:, rows, None] - cum_cols[:, None, :]
        return jnp.where(ok[None], scores, MASKED_SCORE)

    attended, totals = [], []
    for first in range(0, seq_len, block):
        scores = masked_scores(first)
        top = jnp.max(scores, axis=2, keepdims=True)
        weights = jnp.exp(scores - top)
        total = jnp.sum(weights, axis=2, keepdims=True)
        added = jnp.einsum("hij,hjd->hid", weights.astype(bf), v_heads, preferred_element_type=f32)
        attended.append(added / total)
        totals.append(top + jnp.log(total))
    attended = jnp.concatenate(attended, axis=1)
    log_total = jnp.concatenate(totals, axis=1)
    mixed_own = attended.astype(bf).transpose(1, 0, 2).reshape(seq_len, head_cols)
    mixed = lax.all_gather(mixed_own, "wide", axis=1, tiled=True)[:, :D]
    middle = resid + jnp.dot(mixed, w_out, preferred_element_type=f32)
    normed_two, _ = rms_parts(middle)
    ffn_input = (normed_two * gains[1]).astype(bf)
    gate_value = jnp.dot(ffn_input, w_in[0], preferred_element_type=f32)
    up_value = jnp.dot(ffn_input, w_in[1], preferred_element_type=f32)
    gate_sigmoid = jax.nn.sigmoid(gate_value)
    hidden = (gate_value * gate_sigmoid * up_value).astype(bf)

    grad_hidden = matmul_last(all_out_grad, w_down).astype(bf).astype(f32)
    grad_gate = grad_hidden * up_value * gate_sigmoid * (1.0 + gate_value * (1.0 - gate_sigmoid))
    grad_gate = grad_gate.astype(bf)
    grad_up = (grad_hidden * gate_value * gate_sigmoid).astype(bf)
    part_two = matmul_last(grad_gate, w_in[0]) + matmul_last(grad_up, w_in[1])
    grad_two = lax.psum_scatter(
        part_two.astype(bf), "wide", scatter_dimension=0, tiled=True
    ).astype(f32)
    middle_own = own_tokens(middle)
    normed_own, factor_own = rms_parts(middle_own)
    gain_two = jnp.sum(grad_two * normed_own, axis=0)
    grad_middle = out_grad[0].astype(f32) + rms_back(grad_two, gains[1], normed_own, factor_own)
    grad_branch = lax.all_gather(grad_middle.astype(bf), "wide", axis=0, tiled=True)

    out_part = jnp.dot(hidden, w_down, preferred_element_type=f32)
    result = middle_own + lax.psum_scatter(
        out_part.astype(bf), "wide", scatter_dimension=0, tiled=True
    ).astype(f32)

    d_down = matmul_first(hidden, all_out_grad)
    d_in = jnp.stack([matmul_first(ffn_input, grad_gate), matmul_first(ffn_input, grad_up)])
    mixed_part = lax.dynamic_slice_in_dim(mixed, rank * part_rows, part_rows, 1)
    d_out = matmul_first(mixed_part, grad_branch)

    w_out_own = lax.dynamic_slice_in_dim(
        jnp.pad(w_out, ((0, padded - D), (0, 0))), rank * head_cols, head_cols, 0
    )
    grad_mixed = (
        matmul_last(grad_branch, w_out_own).astype(bf).reshape(seq_len, heads, DH).transpose(1, 0, 2)
    )
    delta = jnp.sum(grad_mixed.astype(f32) * attended, axis=2, keepdims=True)
    grad_q, cum_q = [], []
    grad_k = jnp.zeros((heads, seq_len, DH), f32)
    grad_v = jnp.zeros((heads, seq_len, DH), f32)
    cum_k = jnp.zeros((heads, seq_len), f32)
    for first in range(0, seq_len, block):
        rows = slice(first, first + block)
        probs = jnp.exp(masked_scores(first) - log_total[:, rows])
        dprobs = jnp.einsum(
            "hid,hjd->hij", grad_mixed[:, rows], v_heads, preferred_element_type=f32
        )
        dscores = (probs * (dprobs - delta[:, rows])).astype(bf)
        grad_q.append(
            jnp.einsum("hij,hjd->hid", dscores, k_heads, preferred_element_type=f32) * scale
        )
        grad_k += (
            jnp.einsum("hij,hid->hjd", dscores, q_heads[:, rows], preferred_element_type=f32)
            * scale
        )
        grad_v += jnp.einsum(
            "hij,hid->hjd", probs.astype(bf), grad_mixed[:, rows], preferred_element_type=f32
        )
        cum_q.append(jnp.sum(dscores.astype(f32), axis=2))
        cum_k += jnp.sum(dscores.astype(f32), axis=1)
    cum_grad = (jnp.concatenate(cum_q, axis=1) - cum_k).T
    grad_log = open_sum(before_f.T, cum_grad)
    grad_logit = (grad_log * jax.nn.sigmoid(-logits)).astype(bf)
    grad_proj = jnp.concatenate(
        [
            member.astype(bf).transpose(1, 0, 2).reshape(seq_len, head_cols)
            for member in (jnp.concatenate(grad_q, axis=1), grad_k, grad_v)
        ],
        axis=1,
    )
    d_qkv = matmul_first(attn_in, grad_proj)
    d_forget_w = matmul_first(attn_in, grad_logit)
    d_forget_b = jnp.sum(grad_logit.astype(f32), axis=0)
    part_one = matmul_last(grad_proj, w_qkv) + matmul_last(grad_logit, gate_w)
    gain_one = jnp.sum(part_one * normed_one, axis=0)
    grad_one = lax.psum_scatter(
        part_one.astype(bf), "wide", scatter_dimension=0, tiled=True
    ).astype(f32)
    first_own, first_factor = rms_parts(inputs[0].astype(f32))
    grad_input = grad_middle + rms_back(grad_one, gains[0], first_own, first_factor)

    red_down = lax.psum_scatter(d_down, "narrow", scatter_dimension=0, tiled=True)
    red_in = lax.psum_scatter(d_in, "narrow", scatter_dimension=2, tiled=True)
    red_out = lax.psum_scatter(d_out, "narrow", scatter_dimension=0, tiled=True)
    red_qkv = lax.psum_scatter(
        d_qkv.reshape(wide_count, narrow_count, in_rows, 3 * head_cols),
        "narrow",
        scatter_dimension=1,
        tiled=True,
    ).reshape(wide_count, in_rows, 3, head_cols)
    sum_gate_w, sum_gate_b = lax.psum((d_forget_w, d_forget_b), "narrow")
    sum_gains = lax.psum(jnp.stack([gain_one, gain_two]), ("wide", "narrow"))
    local_square = (
        jnp.sum(red_qkv * red_qkv)
        + jnp.sum(red_out * red_out)
        + jnp.sum(red_in * red_in)
        + jnp.sum(red_down * red_down)
        + (jnp.sum(sum_gate_w * sum_gate_w) + jnp.sum(sum_gate_b * sum_gate_b)) / narrow_count
    )
    square_total = lax.psum(local_square, ("wide", "narrow")) + jnp.sum(sum_gains * sum_gains)
    grad_norm = jnp.sqrt(square_total)
    clip_factor = jnp.minimum(1.0, CLIP_NORM / (grad_norm + 1e-06))

    gate_w_all = lax.all_gather(sum_gate_w, "wide", axis=1, tiled=True)[:, :H]
    gate_b_all = lax.all_gather(sum_gate_b, "wide", axis=0, tiled=True)[:H]

    own_qkv = (
        exchange(red_qkv).transpose(2, 1, 0, 3).reshape(3, in_rows, padded)[:, :, :D]
    )

    spare = wide_count - 4
    small_moms = exchange(
        jnp.concatenate(
            [qkv_mom.astype(bf), out_mom.astype(bf)[None], jnp.zeros((spare, in_rows, D), bf)]
        )
    )
    ff_moms = to_groups(
        jnp.stack([in_mom[0].astype(bf).T, in_mom[1].astype(bf).T, down_mom.astype(bf)]),
        4,
        rank,
        wide_count,
    )
    out_grads = exchange(
        jnp.concatenate(
            [
                jnp.zeros((3, in_rows, D), bf),
                red_out.astype(bf)[None],
                jnp.zeros((spare, in_rows, D), bf),
            ]
        )
    )
    ff_grads = to_groups(
        jnp.stack([red_in[0].astype(bf).T, red_in[1].astype(bf).T, red_down.astype(bf)]),
        4,
        rank,
        wide_count,
    )
    qkv_grads = exchange(
        jnp.concatenate(
            [
                red_qkv.astype(bf)
                .transpose(2, 0, 1, 3)
                .reshape(3, wide_count * in_rows, head_cols),
                jnp.zeros((spare + 1, wide_count * in_rows, head_cols), bf),
            ]
        )
    )
    qkv_grads = qkv_grads.transpose(1, 0, 2).reshape(wide_count * in_rows, padded)[:, :D]
    small_own = jnp.where(rank == 3, out_grads.reshape(-1, D), qkv_grads)
    small_mom_own = small_moms.reshape(-1, D)
    ff_own = ff_grads.reshape(-1, D)
    ff_mom_own = ff_moms.reshape(-1, D)
    small_all = lax.all_gather(small_own, "narrow", axis=0, tiled=True)
    small_mom_all = lax.all_gather(small_mom_own, "narrow", axis=0, tiled=True)
    ff_all = lax.all_gather(ff_own, "narrow", axis=0, tiled=True)
    ff_mom_all = lax.all_gather(ff_mom_own, "narrow", axis=0, tiled=True)

    lead_coef = (1.0 + MOMENTUM) * clip_factor
    mom_coef = MOMENTUM * MOMENTUM

    def direction(gradient, moment):
        return (lead_coef * gradient.astype(f32) + mom_coef * moment.astype(f32)).astype(bf)

    holds_ff = (rank >= 4) & (rank < 7)

    def ff_gram(operands):
        rows = direction(operands[2], operands[3])
        return matmul_first(rows, rows)

    def small_gram(operands):
        rows = direction(operands[0], operands[1])
        return matmul_first(rows, rows)

    gram = lax.cond(
        holds_ff, ff_gram, small_gram, (small_all, small_mom_all, ff_all, ff_mom_all)
    )
    norm_square = jnp.sum(gram * jnp.eye(D, dtype=f32))
    inverse = 1.0 / (jnp.sqrt(norm_square) + 1e-07)
    factor = (orthogonal_factor(gram * (inverse * inverse)) * inverse).astype(bf)
    small_ortho = jnp.dot(
        direction(small_own, small_mom_own), factor, preferred_element_type=f32
    ).astype(bf)
    ff_ortho = jnp.dot(
        direction(ff_own, ff_mom_own), factor, preferred_element_type=f32
    ).astype(bf)
    small_back = exchange(small_ortho.reshape(wide_count, in_rows, D))
    ff_back = from_groups(ff_ortho.reshape(wide_count, ff_rows, D), 4, 3, rank, wide_count)
    ortho_qkv = small_back[0:3].astype(f32)
    ortho_out = small_back[3].astype(f32)
    ortho_in = jnp.stack([ff_back[0].T, ff_back[1].T]).astype(f32)
    ortho_down = ff_back[2].astype(f32)

    def moved(moment, gradient):
        return MOMENTUM * moment + clip_factor * gradient

    def stepped(weight, rate, ortho):
        return (1.0 - MUON_DECAY) * weight - rate * ortho

    bias_one = 1.0 - BETA_FIRST**STEP
    bias_two = 1.0 - BETA_SECOND**STEP
    gains_new, gains_first, gains_second = adam_update(
        gains, gains_m, gains_v, clip_factor * sum_gains, bias_one, bias_two, RATE_GAINS
    )
    forget_w_new, forget_w_first, forget_w_second = adam_update(
        fgate_w, fgate_w_m, fgate_w_v, clip_factor * gate_w_all, bias_one, bias_two, RATE_FGATE_W
    )
    forget_b_new, forget_b_first, forget_b_second = adam_update(
        fgate_b, fgate_b_m, fgate_b_v, clip_factor * gate_b_all, bias_one, bias_two, RATE_FGATE_B
    )
    return (
        result.astype(bf)[None],
        grad_input[None],
        grad_norm.reshape(1),
        stepped(qkv_w, tall_rate(D, D, D), ortho_qkv),
        stepped(out_w, tall_rate(D, D, D // 32), ortho_out),
        stepped(ffn_in, tall_rate(FF, D, D), ortho_in),
        stepped(ffn_out, tall_rate(FF, D, FF), ortho_down),
        moved(qkv_mom, own_qkv),
        moved(out_mom, red_out),
        moved(in_mom, red_in),
        moved(down_mom, red_down),
        gains_new,
        gains_first,
        gains_second,
        forget_w_new,
        forget_w_first,
        forget_w_second,
        forget_b_new,
        forget_b_first,
        forget_b_second,
    )


def solution(mesh):
    placed = (
        P("narrow", "wide", None),
        P("narrow", "wide", None),
        P(None, ("wide", "narrow"), None),
        P(("wide", "narrow"), None),
        P(None, None, ("wide", "narrow")),
        P(("wide", "narrow"), None),
        P(None, ("wide", "narrow"), None),
        P(("wide", "narrow"), None),
        P(None, None, ("wide", "narrow")),
        P(("wide", "narrow"), None),
        P(),
        P(),
        P(),
        P(),
        P(),
        P(),
        P(),
        P(),
        P(),
        P("narrow", None),
        P("narrow", None),
        P("narrow", None, None),
    )
    return jax.shard_map(
        shards,
        mesh=mesh,
        in_specs=placed,
        out_specs=(
            P("narrow", "wide", None),
            P("narrow", "wide", None),
            P(),
            P(None, ("wide", "narrow"), None),
            P(("wide", "narrow"), None),
            P(None, None, ("wide", "narrow")),
            P(("wide", "narrow"), None),
            P(None, ("wide", "narrow"), None),
            P(("wide", "narrow"), None),
            P(None, None, ("wide", "narrow")),
            P(("wide", "narrow"), None),
            P(),
            P(),
            P(),
            P(),
            P(),
            P(),
            P(),
            P(),
            P(),
        ),
        check_vma=False,
    )
```
